256 devices in a mesh: level: 4 (over y), gx: 8 (over z_lo, x), gy: 8 (over z_hi, core).
Axes of the slice: x: 4, y: 4, z: 8 (z_hi: 4, z_lo: 2; z = z_hi * 2 + z_lo), core: 2. Of those that a mesh axis runs over, the one named last changes fastest.
Arguments:
- state: float32 [5, 64, 128, 128], P(None, 'gx', 'gy'), may hold values from -0.75 to 5.3, as said below
Outputs:
- level_states: float32 [4, 5, 64, 128, 128], P('level', None, 'gx', 'gy')
The draws below stay inside these ranges and needn't reach their ends.
Inputs may be any that keep to these rules, and one draw needn't show every extreme that they name: state[0] is a density from 1.5 to 3; state[1:4] are the density times velocity components, each velocity component of magnitude at most 0.25; state[4] is the total energy, a pressure from 1 to 2 divided by 0.4 plus the kinetic energy.
All inputs are finite; a program needn't handle non-finite values.
Results may differ from the reference program's by a relative error of at most 0.0001.
Values sent between devices are 32-bit elements; how exact they have to be, the bound alone decides.
A program may use at most 64 MiB of HBM per device.

```python
import math
import jax
import jax.numpy as jnp

NZ = 128
STEPS = 3
NX = 64
NY = 128
N_LEVEL = 4


def draw_state(key, part):
    keys = jax.random.split(jax.random.fold_in(key, 17), 3)
    shape = (NX, NY, NZ)
    specific_volume_inverse = jnp.exp(jax.random.uniform(keys[0], shape, jnp.float32, math.log(1.5), math.log(3.0)))
    normal_stress_scalar = jax.random.uniform(keys[1], shape, jnp.float32, 1.0, 2.0)
    velocity = jax.random.uniform(keys[2], (3,) + shape, jnp.float32, -0.25, 0.25)
    momentum = specific_volume_inverse[None] * velocity
    energy = normal_stress_scalar / 0.4 + 0.5 * specific_volume_inverse * jnp.sum(velocity * velocity, axis=0)
    return jnp.concatenate([specific_volume_inverse[None], momentum, energy[None]], axis=0).astype(jnp.float32)


def setup_inputs(seed: int = 0) -> dict:
    splits = jax.random.split(jax.random.key(seed), 2)
    return {
        "state": draw_state(jax.random.fold_in(splits[1], 71), 0),
    }


DT = 0.1
GAMMA = 1.4
SHEAR_COEFFICIENT = 0.1
CONDUCTIVITY = 0.1
FIRST_COEF = (4.0 / 5.0, -1.0 / 5.0, 4.0 / 105.0, -1.0 / 280.0)
SECOND_CENTER = -205.0 / 72.0
SECOND_COEF = (8.0 / 5.0, -1.0 / 5.0, 8.0 / 315.0, -1.0 / 560.0)


def shifted(quantity, direction, offset):
    extent = quantity.shape[-3:]
    picks = [slice(4, extent[0] - 4), slice(4, extent[1] - 4), slice(4, extent[2] - 4)]
    picks[direction] = slice(4 + offset, extent[direction] - 4 + offset)
    leading = (slice(None),) * (quantity.ndim - 3)
    return quantity[leading + tuple(picks)]


def first_derivative(quantity, direction):
    total = 0.0
    for position, weight in enumerate(FIRST_COEF):
        total = total + weight * (shifted(quantity, direction, position + 1) - shifted(quantity, direction, -position - 1))
    return total


def second_derivative_sum(quantity):
    total = 0.0
    for direction in range(3):
        total = total + SECOND_CENTER * shifted(quantity, direction, 0)
        for position, weight in enumerate(SECOND_COEF):
            total = total + weight * (shifted(quantity, direction, position + 1) + shifted(quantity, direction, -position - 1))
    return total


def tendency(padded):
    specific_volume_inverse = padded[0]
    momentum = padded[1:4]
    energy = padded[4]
    velocity = momentum / specific_volume_inverse
    kinetic_energy_share = 0.5 * jnp.sum(velocity * velocity, axis=0)
    normal_stress_scalar = (GAMMA - 1.0) * (energy - specific_volume_inverse * kinetic_energy_share)
    absolute_kelvin_value = normal_stress_scalar / specific_volume_inverse
    divergence = 0.0
    for direction in range(3):
        along = velocity[direction]
        rows = [momentum[component] * along + (normal_stress_scalar if component == direction else 0.0) for component in range(3)]
        flux = jnp.stack([momentum[direction]] + rows + [(energy + normal_stress_scalar) * along])
        divergence = divergence + first_derivative(flux, direction)
    viscous = SHEAR_COEFFICIENT * second_derivative_sum(velocity)
    conduction_contribution = SHEAR_COEFFICIENT * second_derivative_sum(kinetic_energy_share) + CONDUCTIVITY * second_derivative_sum(absolute_kelvin_value)
    return jnp.concatenate([-divergence[0:1], viscous - divergence[1:4], (conduction_contribution - divergence[4])[None]], axis=0)


def reference(state):
    finals = []
    history = None
    for level_number in range(N_LEVEL):
        nodes = STEPS + 1 if level_number < N_LEVEL - 1 else STEPS
        current = state
        record = []
        for node in range(nodes):
            padded = jnp.pad(current, ((0, 0), (4, 4), (4, 4), (4, 4)), mode="wrap")
            forcing = tendency(padded)
            record.append(forcing)
            if node < STEPS:
                if history is None:
                    current = current + DT * forcing
                else:
                    if node == 0:
                        quad_term = 0.5 * (history[0] + history[1])
                    else:
                        quad_term = (8.0 * history[node] + 5.0 * history[node + 1] - history[node - 1]) / 12.0
                    current = current + DT * (forcing - history[node] + quad_term)
        finals.append(current)
        history = record
    return jnp.stack(finals)
```

```python
import jax
import jax.numpy as jnp
from jax import lax
from jax.experimental import pallas as pl
from jax.experimental.pallas import tpu as pltpu
from jax.sharding import PartitionSpec as P

DT = 0.1
A1 = (4.0 / 5.0, -1.0 / 5.0, 4.0 / 105.0, -1.0 / 280.0)
B0 = -205.0 / 72.0
B1 = (8.0 / 5.0, -1.0 / 5.0, 8.0 / 315.0, -1.0 / 560.0)
MU = 0.1

S, U01, U02, U03, U21, U31, U22, U13, U32, U23, U11, U12 = range(12)
SENT = 10
F0, TA1, TA2, TA3, TB1, TB2, TB3, TC1, TC2, TC3, TD1, TD2 = range(12)


def tendency(xe, yh):
    own = slice(4, 8)
    u = [jnp.concatenate([xe[i], yh[i]], axis=0) for i in range(5)]
    rho, m, e = u[0], u[1:4], u[4]
    inv = 1.0 / rho
    v = [mi * inv for mi in m]
    k = 0.5 * (v[0] * v[0] + v[1] * v[1] + v[2] * v[2])
    p = 0.4 * (e - rho * k)
    q = k + p * inv
    h = e + p
    diffused = [None, v[0], v[1], v[2], q]

    def flux(direction, part):
        along = part(v[direction])
        rows = [part(m[i]) * along + (part(p) if i == direction else 0.0) for i in range(3)]
        return [part(m[direction])] + rows + [part(h) * along]

    row = lax.broadcasted_iota(jnp.int32, (4, 8, 128), 1)
    ends_y = {}
    for w in (1, 2, 3, 4):
        ends_y[w] = (row < w, row >= 8 - w)

    def x_shifts(a, w):
        return a[4 + w : 8 + w], a[4 - w : 8 - w]

    def y_shifts(a, w):
        mine, other = a
        up = pltpu.roll(jnp.where(ends_y[w][0], other, mine), 8 - w, 1)
        down = pltpu.roll(jnp.where(ends_y[w][1], other, mine), w, 1)
        return up, down

    def z_shifts(a, w):
        return pltpu.roll(a, 128 - w, 2), pltpu.roll(a, w, 2)

    def xpart(a):
        return a[0:12]

    def ypart(a):
        return a[4:8], a[12:16]

    flux_x = flux(0, xpart)
    flux_ym = flux(1, lambda a: a[4:8])
    flux_yo = flux(1, lambda a: a[12:16])
    flux_z = flux(2, lambda a: a[4:8])
    out = []
    for c in range(5):
        total = None
        if diffused[c] is not None:
            total = (3.0 * MU * B0) * diffused[c][own]
        for shifts, f, part in (
            (x_shifts, flux_x[c], xpart),
            (y_shifts, (flux_ym[c], flux_yo[c]), ypart),
            (z_shifts, flux_z[c], lambda a: a[4:8]),
        ):
            for w in (1, 2, 3, 4):
                up, down = shifts(f, w)
                term = (-A1[w - 1]) * (up - down)
                total = term if total is None else total + term
                if diffused[c] is not None:
                    up, down = shifts(part(diffused[c]), w)
                    total = total + (MU * B1[w - 1]) * (up + down)
        out.append(total)
    return out


def kernel(nx, nzh, state, out, xe, ry, sy, yh, g, fin, load_sem, in_sem, send_sem, recv_sem, osend_sem, orecv_sem):
    y = lax.axis_index("level")
    gx = lax.axis_index("gx")
    gy = lax.axis_index("gy")
    zh, c = gy // 2, gy % 2
    pos = y + (zh % 2) * (3 - 2 * y)
    half, rows = pos // 2, pl.multiple_of((pos % 2) * 8, 8)
    nyi = 4 * nzh
    yi = zh * 4 + pos

    def at_y(index):
        zh2, pos2 = index // 4, index % 4
        return (pos2 + (zh2 % 2) * (3 - 2 * pos2), gx, zh2 * 2 + c)

    up_x = (y, (gx + c) % nx, zh * 2 + 1 - c)
    down_x = (y, (gx + nx - 1 + c) % nx, zh * 2 + 1 - c)
    up_y = at_y((yi + 1) % nyi)
    down_y = at_y((yi + nyi - 1) % nyi)
    partner = (y, gx, zh * 2 + 1 - c)
    outer_x = (y, (gx + nx + 2 * c - 1) % nx, zh * 2 + 1 - c)

    barrier = pltpu.get_barrier_semaphore()
    peers = [outer_x, up_y, down_y, partner]
    for d in (1, 2, 3):
        for core in (0, 1):
            peers.append(((y + d) % 4, gx, zh * 2 + core))
    for peer in peers:
        pl.semaphore_signal(barrier, inc=1, device_id=peer, device_id_type=pl.DeviceIdType.MESH)

    def piece(core):
        return state.at[:, pl.ds(4 * core, 4), pl.ds(rows, 8), :]

    own = xe.at[S, :, pl.ds(4, 4)]
    load = pltpu.make_async_copy(piece(c), own, load_sem)
    give = pltpu.make_async_remote_copy(
        src_ref=piece(1 - c),
        dst_ref=own,
        send_sem=osend_sem.at[4],
        recv_sem=in_sem,
        device_id=partner,
        device_id_type=pl.DeviceIdType.MESH,
    )

    @pl.when(c == half)
    def _():
        load.start()

    pl.semaphore_wait(barrier, len(peers))

    @pl.when(c == half)
    def _():
        give.start()
        load.wait()

    @pl.when(c != half)
    def _():
        give.wait_recv()

    def copies(slot):
        mine = xe.at[slot, :, pl.ds(4, 4)]
        ends = (
            (sy.at[slot, 1], ry.at[slot, 1], up_y),
            (sy.at[slot, 0], ry.at[slot, 0], down_y),
            (mine, xe.at[slot, :, pl.ds(0, 4)], up_x),
            (mine, xe.at[slot, :, pl.ds(8, 4)], down_x),
        )
        return [
            pltpu.make_async_remote_copy(
                src_ref=src,
                dst_ref=dst,
                send_sem=send_sem.at[slot, i],
                recv_sem=recv_sem.at[slot, i],
                device_id=device,
                device_id_type=pl.DeviceIdType.MESH,
            )
            for i, (src, dst, device) in enumerate(ends)
        ]

    def send(slot, value=None):
        for i in range(5):
            if value is None:
                a = xe[slot, i, 4:8]
            else:
                a = value[i]
                xe[slot, i, 4:8] = a
            sy[slot, 0, i] = a[:, 0:4]
            sy[slot, 1, i] = a[:, 4:8]
        for copy in copies(slot):
            copy.start()

    def receive(slot):
        for copy in copies(slot):
            copy.wait_recv()
        for i in range(5):
            yh[slot, i] = jnp.concatenate([ry[slot, 0, i], ry[slot, 1, i]], axis=1)

    def evaluate(slot, into):
        result = tendency([xe[slot, i] for i in range(5)], [yh[slot, i] for i in range(5)])
        for i in range(5):
            g[into, i] = result[i]

    def mix(terms):
        parts = []
        for i in range(5):
            total = None
            for kind, slot, factor in terms:
                a = xe[slot, i, 4:8] if kind == "u" else g[slot, i]
                a = a if factor == 1.0 else factor * a
                total = a if total is None else total + a
            parts.append(total)
        return parts

    def everywhere(slot, terms):
        for ref in (xe, yh):
            for i in range(5):
                total = None
                for source, factor in terms:
                    a = factor * ref[source, i]
                    total = a if total is None else total + a
                ref[slot, i] = total

    def place(level):
        return out.at[0, :, pl.ds(4 * c, 4), pl.ds(rows, 8), :]

    def final(level, src):
        piece_sem = orecv_sem.at[(pos % 2) * 2 + c]
        here = jnp.logical_and(y == level, c == half)
        away = pltpu.make_async_remote_copy(
            src_ref=src,
            dst_ref=place(level),
            send_sem=osend_sem.at[level],
            recv_sem=piece_sem,
            device_id=(level, gx, zh * 2 + half),
            device_id_type=pl.DeviceIdType.MESH,
        )
        local = pltpu.make_async_copy(src, place(level), piece_sem)

        @pl.when(here)
        def _():
            local.start()

        @pl.when(jnp.logical_not(here))
        def _():
            away.start()

        return here, away

    send(S)
    receive(S)
    evaluate(S, F0)
    send(U01, mix([("u", S, 1.0), ("g", F0, DT)]))
    receive(U01)
    evaluate(U01, TA1)
    send(U02, mix([("u", U01, 1.0), ("g", TA1, DT)]))
    receive(U02)
    evaluate(U02, TA2)
    send(U03, mix([("u", U02, 1.0), ("g", TA2, DT)]))
    everywhere(U11, [(S, 0.5), (U02, 0.5)])
    evaluate(U11, TB1)
    send(U21, mix([("u", S, 1.0), ("g", F0, 0.5 * DT), ("g", TB1, 0.5 * DT)]))
    finals = [final(0, xe.at[U03, :, pl.ds(4, 4)])]
    receive(U03)
    evaluate(U03, TA3)
    receive(U21)
    evaluate(U21, TC1)
    send(U31, mix([("u", S, 1.0), ("g", F0, 0.5 * DT), ("g", TC1, 0.5 * DT)]))
    everywhere(U12, [(S, -5 / 12), (U01, -9 / 12), (U02, -3 / 12), (U03, 5 / 12), (U21, 2.0)])
    evaluate(U12, TB2)
    send(
        U22,
        mix(
            [("u", U21, 1.0), ("g", TC1, DT), ("g", TB1, -4 / 12 * DT), ("g", TB2, 5 / 12 * DT), ("g", F0, -1 / 12 * DT)]
        ),
    )
    send(
        U13,
        mix(
            [("u", U12, 1.0), ("g", TB2, DT), ("g", TA2, -4 / 12 * DT), ("g", TA3, 5 / 12 * DT), ("g", TA1, -1 / 12 * DT)]
        ),
    )
    finals.append(final(1, xe.at[U13, :, pl.ds(4, 4)]))
    receive(U31)
    evaluate(U31, TD1)
    receive(U22)
    evaluate(U22, TC2)
    send(
        U32,
        mix(
            [("u", U31, 1.0), ("g", TD1, DT), ("g", TC1, -4 / 12 * DT), ("g", TC2, 5 / 12 * DT), ("g", F0, -1 / 12 * DT)]
        ),
    )
    receive(U13)
    evaluate(U13, TB3)
    send(
        U23,
        mix(
            [("u", U22, 1.0), ("g", TC2, DT), ("g", TB2, -4 / 12 * DT), ("g", TB3, 5 / 12 * DT), ("g", TB1, -1 / 12 * DT)]
        ),
    )
    finals.append(final(2, xe.at[U23, :, pl.ds(4, 4)]))
    receive(U32)
    evaluate(U32, TD2)
    receive(U23)
    evaluate(U23, TC3)
    last = mix(
        [("u", U32, 1.0), ("g", TD2, DT), ("g", TC2, -4 / 12 * DT), ("g", TC3, 5 / 12 * DT), ("g", TC1, -1 / 12 * DT)]
    )
    for i in range(5):
        fin[i] = last[i]
    finals.append(final(3, fin))

    for slot in range(SENT):
        for copy in copies(slot):
            copy.wait_send()
    for here, away in finals:

        @pl.when(jnp.logical_not(here))
        def _(away=away):
            away.wait_send()

    @pl.when(c == half)
    def _():
        give.wait_send()

    for i in range(4):
        pltpu.make_async_copy(fin, place(3), orecv_sem.at[i]).wait()


def solution(mesh):
    nx, nzh = mesh.shape["gx"], mesh.shape["gy"] // 2

    def body(state):
        f32 = jnp.float32
        return pl.pallas_call(
            lambda *refs: kernel(nx, nzh, *refs),
            out_shape=jax.ShapeDtypeStruct((1,) + state.shape, f32),
            in_specs=[pl.BlockSpec(memory_space=pl.ANY)],
            out_specs=pl.BlockSpec(memory_space=OUT_SPACE),
            scratch_shapes=[
                pltpu.VMEM((12, 5, 12, 8, 128), f32),
                pltpu.VMEM((SENT, 2, 5, 4, 4, 128), f32),
                pltpu.VMEM((SENT, 2, 5, 4, 4, 128), f32),
                pltpu.VMEM((12, 5, 4, 8, 128), f32),
                pltpu.VMEM((12, 5, 4, 8, 128), f32),
                pltpu.VMEM((5, 4, 8, 128), f32),
                pltpu.SemaphoreType.DMA,
                pltpu.SemaphoreType.DMA,
                pltpu.SemaphoreType.DMA((SENT, 4)),
                pltpu.SemaphoreType.DMA((SENT, 4)),
                pltpu.SemaphoreType.DMA((5,)),
                pltpu.SemaphoreType.DMA((4,)),
            ],
            compiler_params=pltpu.CompilerParams(collective_id=0, has_side_effects=True),
            name="window",
        )(state)

    return jax.shard_map(
        body,
        mesh=mesh,
        in_specs=(P(None, "gx", "gy", None),),
        out_specs=P("level", None, "gx", "gy", None),
        check_vma=False,
    )


OUT_SPACE = pltpu.VMEM
```

```python
import jax
import jax.numpy as jnp
from jax import lax
from jax.experimental import pallas as pl
from jax.experimental.pallas import tpu as pltpu
from jax.sharding import PartitionSpec as P

DT = 0.1
A1 = (4.0 / 5.0, -1.0 / 5.0, 4.0 / 105.0, -1.0 / 280.0)
B0 = -205.0 / 72.0
B1 = (8.0 / 5.0, -1.0 / 5.0, 8.0 / 315.0, -1.0 / 560.0)
MU = 0.1

S, U01, U02, U03, U21, U31, U22, U13, U32, U23, U11, U12 = range(12)
SENT = 10
F0, TA1, TA2, TA3, TB1, TB2, TB3, TC1, TC2, TC3, TD1, TD2 = range(12)


def primitives(u):
    rho, m, e = u[0], u[1:4], u[4]
    inv = 1.0 / rho
    v = [mi * inv for mi in m]
    k = 0.5 * (v[0] * v[0] + v[1] * v[1] + v[2] * v[2])
    p = 0.4 * (e - rho * k)
    return m, v, p, e + p, k + p * inv


def flux(parts, d):
    m, v, p, h, _ = parts
    return [m[d]] + [m[i] * v[d] + p if i == d else m[i] * v[d] for i in range(3)] + [h * v[d]]


def diffused(parts):
    return [None, *parts[1], parts[4]]


def along(total, f, w, shifts):
    for n in (1, 2, 3, 4):
        up, down = shifts(f, n)
        term = (-A1[n - 1]) * (up - down)
        total = term if total is None else total + term
        if w is not None:
            up, down = shifts(w, n)
            total = total + (MU * B1[n - 1]) * (up + down)
    return total


def inner(u):
    parts = primitives(u)
    out = []
    for f, w in zip(flux(parts, 2), diffused(parts)):
        total = None if w is None else (3.0 * MU * B0) * w
        out.append(along(total, f, w, lambda a, n: (pltpu.roll(a, 128 - n, 2), pltpu.roll(a, n, 2))))
    return parts, out


def outer(state, low, high, ends):
    parts, out = state
    row = lax.broadcasted_iota(jnp.int32, (4, 8, 128), 1)
    before, after, edge = primitives(low), primitives(high), primitives(ends)

    def join(a, b, c):
        return None if b is None else jnp.concatenate([a, b, c], axis=0)

    fx = [join(*t) for t in zip(flux(before, 0), flux(parts, 0), flux(after, 0))]
    wx = [join(*t) for t in zip(diffused(before), diffused(parts), diffused(after))]
    out = [along(t, f, w, lambda a, n: (a[4 + n : 8 + n], a[4 - n : 8 - n])) for t, f, w in zip(out, fx, wx)]

    def y_shifts(a, n):
        mine, other = a
        up = pltpu.roll(jnp.where(row < n, other, mine), 8 - n, 1)
        down = pltpu.roll(jnp.where(row >= 8 - n, other, mine), n, 1)
        return up, down

    fy = zip(flux(parts, 1), flux(edge, 1))
    wy = [None if a is None else (a, b) for a, b in zip(diffused(parts), diffused(edge))]
    return [along(t, f, w, y_shifts) for t, f, w in zip(out, fy, wy)]


def kernel(nxp, nzh, state, out, xe, ry, sy, yh, g, fin, in_sem, send_sem, recv_sem, osend_sem, orecv_sem):
    y = lax.axis_index("level")
    gx = lax.axis_index("gx")
    gy = lax.axis_index("gy")
    h, c = gy // 2, gy % 2
    x, lo = gx % nxp, gx // nxp
    q = y // 2
    back = ((y + 1) // 2 + 1) % 2
    mine_x = back * nxp + x
    pos = q + lo * (3 - 2 * q)
    rows = pl.multiple_of((pos % 2) * 8, 8)
    nyi = 4 * nzh

    def owner(column, index, core):
        h2, pos2 = index // 4, index % 4
        lo2 = pos2 // 2
        q2 = pos2 + lo2 * (3 - 2 * pos2)
        return (1 + q2 + (column // nxp) * (2 * q2 - 1), lo2 * nxp + column % nxp, h2 * 2 + core)

    yi = h * 4 + pos
    nx = 2 * nxp
    up_x = owner((mine_x + c) % nx, yi, 1 - c)
    down_x = owner((mine_x + nx - 1 + c) % nx, yi, 1 - c)
    up_y = owner(mine_x, (yi + 1) % nyi, c)
    down_y = owner(mine_x, (yi + nyi - 1) % nyi, c)
    outer_x = owner((mine_x + nx + 2 * c - 1) % nx, yi, 1 - c)

    barrier = pltpu.get_barrier_semaphore()
    peers = [outer_x, up_y, down_y]
    for d in range(16):
        if d:
            peers.append(((y + d // 4) % 4, ((lo + d // 2 % 2) % 2) * nxp + x, h * 2 + (c + d) % 2))
    for peer in peers:
        pl.semaphore_signal(barrier, inc=1, device_id=peer, device_id_type=pl.DeviceIdType.MESH)

    own = xe.at[S, :, pl.ds(4, 4)]
    give_pos = q + c * (3 - 2 * q)
    holder = lo == back
    gives = []
    for core in (0, 1):
        src = state.at[:, pl.ds(4 * core, 4), pl.ds(pl.multiple_of((give_pos % 2) * 8, 8), 8), :]
        away = pltpu.make_async_remote_copy(
            src_ref=src,
            dst_ref=own,
            send_sem=osend_sem.at[4 + core],
            recv_sem=in_sem,
            device_id=(y, c * nxp + x, h * 2 + core),
            device_id_type=pl.DeviceIdType.MESH,
        )
        here = jnp.logical_and(c == lo, c == core)
        gives.append((here, away, pltpu.make_async_copy(src, own, in_sem)))

    pl.semaphore_wait(barrier, len(peers))

    @pl.when(holder)
    def _():
        for here, away, local in gives:
            pl.when(here)(local.start)
            pl.when(jnp.logical_not(here))(away.start)

    gives[0][2].wait()

    def copies(slot):
        mine = xe.at[slot, :, pl.ds(4, 4)]
        ends = (
            (mine, xe.at[slot, :, pl.ds(0, 4)], up_x),
            (mine, xe.at[slot, :, pl.ds(8, 4)], down_x),
            (sy.at[slot, 1], ry.at[slot, 1], up_y),
            (sy.at[slot, 0], ry.at[slot, 0], down_y),
        )
        return [
            pltpu.make_async_remote_copy(
                src_ref=src,
                dst_ref=dst,
                send_sem=send_sem.at[slot, i],
                recv_sem=recv_sem.at[slot, i],
                device_id=device,
                device_id_type=pl.DeviceIdType.MESH,
            )
            for i, (src, dst, device) in enumerate(ends)
        ]

    def send(slot, value=None):
        along = copies(slot)
        if value is None:
            value = [xe[slot, i, 4:8] for i in range(5)]
        else:
            for i in range(5):
                xe[slot, i, 4:8] = value[i]
        for copy in along[:2]:
            copy.start()
        for i in range(5):
            sy[slot, 0, i] = value[i][:, 0:4]
            sy[slot, 1, i] = value[i][:, 4:8]
        for copy in along[2:]:
            copy.start()

    def receive(slot):
        for copy in copies(slot):
            copy.wait_recv()
        for i in range(5):
            yh[slot, i] = jnp.concatenate([ry[slot, 0, i], ry[slot, 1, i]], axis=1)

    def begin(slot):
        return inner([xe[slot, i, 4:8] for i in range(5)])

    def evaluate(slot, into, begun):
        result = outer(begun, *([ref[slot, i, part] for i in range(5)] for ref, part in ((xe, slice(0, 4)), (xe, slice(8, 12)), (yh, slice(0, 4)))))
        for i in range(5):
            g[into, i] = result[i]

    def mix(terms):
        parts = []
        for i in range(5):
            total = None
            for kind, slot, factor in terms:
                a = xe[slot, i, 4:8] if kind == "u" else g[slot, i]
                a = a if factor == 1.0 else factor * a
                total = a if total is None else total + a
            parts.append(total)
        return parts

    def everywhere(slot, terms):
        for ref in (xe, yh):
            for i in range(5):
                total = None
                for source, factor in terms:
                    a = factor * ref[source, i]
                    total = a if total is None else total + a
                ref[slot, i] = total

    def place(level):
        return out.at[0, :, pl.ds(4 * c, 4), pl.ds(rows, 8), :]

    def final(level, src):
        piece_sem = orecv_sem.at[(pos % 2) * 2 + c]
        here = jnp.logical_and(jnp.logical_and(y == level, c == lo), lo == back)
        away = pltpu.make_async_remote_copy(
            src_ref=src,
            dst_ref=place(level),
            send_sem=osend_sem.at[level],
            recv_sem=piece_sem,
            device_id=(level, mine_x, h * 2 + lo),
            device_id_type=pl.DeviceIdType.MESH,
        )
        local = pltpu.make_async_copy(src, place(level), piece_sem)

        @pl.when(here)
        def _():
            local.start()

        @pl.when(jnp.logical_not(here))
        def _():
            away.start()

        return here, away

    send(S)
    begun = begin(S)
    receive(S)
    evaluate(S, F0, begun)
    send(U01, mix([("u", S, 1.0), ("g", F0, DT)]))
    begun = begin(U01)
    receive(U01)
    evaluate(U01, TA1, begun)
    send(U02, mix([("u", U01, 1.0), ("g", TA1, DT)]))
    begun = begin(U02)
    receive(U02)
    evaluate(U02, TA2, begun)
    send(U03, mix([("u", U02, 1.0), ("g", TA2, DT)]))
    everywhere(U11, [(S, 0.5), (U02, 0.5)])
    evaluate(U11, TB1, begin(U11))
    send(U21, mix([("u", S, 1.0), ("g", F0, 0.5 * DT), ("g", TB1, 0.5 * DT)]))
    finals = [final(0, xe.at[U03, :, pl.ds(4, 4)])]
    begun = begin(U03), begin(U21)
    receive(U03)
    evaluate(U03, TA3, begun[0])
    receive(U21)
    evaluate(U21, TC1, begun[1])
    send(U31, mix([("u", S, 1.0), ("g", F0, 0.5 * DT), ("g", TC1, 0.5 * DT)]))
    everywhere(U12, [(S, -5 / 12), (U01, -9 / 12), (U02, -3 / 12), (U03, 5 / 12), (U21, 2.0)])
    evaluate(U12, TB2, begin(U12))
    send(
        U22,
        mix(
            [("u", U21, 1.0), ("g", TC1, DT), ("g", TB1, -4 / 12 * DT), ("g", TB2, 5 / 12 * DT), ("g", F0, -1 / 12 * DT)]
        ),
    )
    send(
        U13,
        mix(
            [("u", U12, 1.0), ("g", TB2, DT), ("g", TA2, -4 / 12 * DT), ("g", TA3, 5 / 12 * DT), ("g", TA1, -1 / 12 * DT)]
        ),
    )
    finals.append(final(1, xe.at[U13, :, pl.ds(4, 4)]))
    begun = begin(U31), begin(U22), begin(U13)
    receive(U31)
    evaluate(U31, TD1, begun[0])
    receive(U22)
    evaluate(U22, TC2, begun[1])
    send(
        U32,
        mix(
            [("u", U31, 1.0), ("g", TD1, DT), ("g", TC1, -4 / 12 * DT), ("g", TC2, 5 / 12 * DT), ("g", F0, -1 / 12 * DT)]
        ),
    )
    receive(U13)
    evaluate(U13, TB3, begun[2])
    send(
        U23,
        mix(
            [("u", U22, 1.0), ("g", TC2, DT), ("g", TB2, -4 / 12 * DT), ("g", TB3, 5 / 12 * DT), ("g", TB1, -1 / 12 * DT)]
        ),
    )
    finals.append(final(2, xe.at[U23, :, pl.ds(4, 4)]))
    begun = begin(U32), begin(U23)
    receive(U32)
    evaluate(U32, TD2, begun[0])
    receive(U23)
    evaluate(U23, TC3, begun[1])
    last = mix(
        [("u", U32, 1.0), ("g", TD2, DT), ("g", TC2, -4 / 12 * DT), ("g", TC3, 5 / 12 * DT), ("g", TC1, -1 / 12 * DT)]
    )
    for i in range(5):
        fin[i] = last[i]
    finals.append(final(3, fin))

    for slot in range(SENT):
        for copy in copies(slot):
            copy.wait_send()
    for here, away in finals:

        @pl.when(jnp.logical_not(here))
        def _(away=away):
            away.wait_send()

    @pl.when(holder)
    def _():
        for here, away, _ in gives:
            pl.when(jnp.logical_not(here))(away.wait_send)

    for i in range(4):
        pltpu.make_async_copy(fin, place(3), orecv_sem.at[i]).wait()


def solution(mesh):
    nxp, nzh = mesh.shape["gx"] // 2, mesh.shape["gy"] // 2

    def body(state):
        f32 = jnp.float32
        return pl.pallas_call(
            lambda *refs: kernel(nxp, nzh, *refs),
            out_shape=jax.ShapeDtypeStruct((1,) + state.shape, f32),
            in_specs=[pl.BlockSpec(memory_space=pltpu.HBM)],
            out_specs=pl.BlockSpec(memory_space=OUT_SPACE),
            scratch_shapes=[
                pltpu.VMEM((12, 5, 12, 8, 128), f32),
                pltpu.VMEM((SENT, 2, 5, 4, 4, 128), f32),
                pltpu.VMEM((SENT, 2, 5, 4, 4, 128), f32),
                pltpu.VMEM((12, 5, 4, 8, 128), f32),
                pltpu.VMEM((12, 5, 4, 8, 128), f32),
                pltpu.VMEM((5, 4, 8, 128), f32),
                pltpu.SemaphoreType.DMA,
                pltpu.SemaphoreType.DMA((SENT, 4)),
                pltpu.SemaphoreType.DMA((SENT, 4)),
                pltpu.SemaphoreType.DMA((6,)),
                pltpu.SemaphoreType.DMA((4,)),
            ],
            compiler_params=pltpu.CompilerParams(collective_id=0, vmem_limit_bytes=24 * 2**20, has_side_effects=True),
            name="window",
        )(state)

    return jax.shard_map(
        body,
        mesh=mesh,
        in_specs=(P(None, "gx", "gy", None),),
        out_specs=P("level", None, "gx", "gy", None),
        check_vma=False,
    )


OUT_SPACE = pl.ANY
```

```python
import jax
import jax.numpy as jnp
from jax import lax
from jax.experimental import pallas as pl
from jax.experimental.pallas import tpu as pltpu
from jax.sharding import PartitionSpec as P

DT = 0.1
A1 = (4.0 / 5.0, -1.0 / 5.0, 4.0 / 105.0, -1.0 / 280.0)
B0 = -205.0 / 72.0
B1 = (8.0 / 5.0, -1.0 / 5.0, 8.0 / 315.0, -1.0 / 560.0)
MU = 0.1

S, U01, U02, U03, U21, U31, U22, U13, U32, U23, U11, U12 = range(12)
SENT = 10
F0, TA1, TA2, TA3, TB1, TB2, TB3, TC1, TC2, TC3, TD1, TD2 = range(12)


def primitives(u):
    rho, m, e = u[0], u[1:4], u[4]
    inv = 1.0 / rho
    v = [mi * inv for mi in m]
    k = 0.5 * (v[0] * v[0] + v[1] * v[1] + v[2] * v[2])
    p = 0.4 * (e - rho * k)
    return m, v, p, e + p, k + p * inv


def flux(parts, d):
    m, v, p, h, _ = parts
    return [m[d]] + [m[i] * v[d] + p if i == d else m[i] * v[d] for i in range(3)] + [h * v[d]]


def diffused(parts):
    return [None, *parts[1], parts[4]]


def along(total, f, w, shifts):
    for n in (1, 2, 3, 4):
        up, down = shifts(f, n)
        term = (-A1[n - 1]) * (up - down)
        total = term if total is None else total + term
        if w is not None:
            up, down = shifts(w, n)
            total = total + (MU * B1[n - 1]) * (up + down)
    return total


def inner(u):
    parts = primitives(u)
    out = []
    for f, w in zip(flux(parts, 2), diffused(parts)):
        total = None if w is None else (3.0 * MU * B0) * w
        out.append(along(total, f, w, lambda a, n: (pltpu.roll(a, 128 - n, 2), pltpu.roll(a, n, 2))))
    return parts, out


def outer(state, low, high, ends):
    parts, out = state
    row = lax.broadcasted_iota(jnp.int32, (4, 8, 128), 1)
    before, after, edge = primitives(low), primitives(high), primitives(ends)

    def join(a, b, c):
        return None if b is None else jnp.concatenate([a, b, c], axis=0)

    fx = [join(*t) for t in zip(flux(before, 0), flux(parts, 0), flux(after, 0))]
    wx = [join(*t) for t in zip(diffused(before), diffused(parts), diffused(after))]
    out = [along(t, f, w, lambda a, n: (a[4 + n : 8 + n], a[4 - n : 8 - n])) for t, f, w in zip(out, fx, wx)]

    def y_shifts(a, n):
        mine, other = a
        up = pltpu.roll(jnp.where(row < n, other, mine), 8 - n, 1)
        down = pltpu.roll(jnp.where(row >= 8 - n, other, mine), n, 1)
        return up, down

    fy = zip(flux(parts, 1), flux(edge, 1))
    wy = [None if a is None else (a, b) for a, b in zip(diffused(parts), diffused(edge))]
    return [along(t, f, w, y_shifts) for t, f, w in zip(out, fy, wy)]


def kernel(nxp, nzh, state, out, xe, ry, sy, yh, g, fin, in_sem, send_sem, recv_sem, osend_sem, orecv_sem):
    y = lax.axis_index("level")
    gx = lax.axis_index("gx")
    gy = lax.axis_index("gy")
    h, c = gy // 2, gy % 2
    x, lo = gx % nxp, gx // nxp
    q = y // 2
    back = ((y + 1) // 2 + 1) % 2
    mine_x = back * nxp + x
    pos = q + lo * (3 - 2 * q)
    rows = pl.multiple_of((pos % 2) * 8, 8)
    nyi = 4 * nzh

    def owner(column, index, core):
        h2, pos2 = index // 4, index % 4
        lo2 = pos2 // 2
        q2 = pos2 + lo2 * (3 - 2 * pos2)
        return (1 + q2 + (column // nxp) * (2 * q2 - 1), lo2 * nxp + column % nxp, h2 * 2 + core)

    yi = h * 4 + pos
    nx = 2 * nxp
    up_x = owner((mine_x + c) % nx, yi, 1 - c)
    down_x = owner((mine_x + nx - 1 + c) % nx, yi, 1 - c)
    up_y = owner(mine_x, (yi + 1) % nyi, c)
    down_y = owner(mine_x, (yi + nyi - 1) % nyi, c)
    outer_x = owner((mine_x + nx + 2 * c - 1) % nx, yi, 1 - c)

    barrier = pltpu.get_barrier_semaphore()
    peers = [outer_x, up_y, down_y]
    for d in range(16):
        if d:
            peers.append(((y + d // 4) % 4, ((lo + d // 2 % 2) % 2) * nxp + x, h * 2 + (c + d) % 2))
    for peer in peers:
        pl.semaphore_signal(barrier, inc=1, device_id=peer, device_id_type=pl.DeviceIdType.MESH)

    own = xe.at[S, :, pl.ds(4, 4)]
    give_pos = q + c * (3 - 2 * q)
    holder = lo == back
    gives = []
    for core in (0, 1):
        src = state.at[:, pl.ds(4 * core, 4), pl.ds(pl.multiple_of((give_pos % 2) * 8, 8), 8), :]
        away = pltpu.make_async_remote_copy(
            src_ref=src,
            dst_ref=own,
            send_sem=osend_sem.at[4 + core],
            recv_sem=in_sem,
            device_id=(y, c * nxp + x, h * 2 + core),
            device_id_type=pl.DeviceIdType.MESH,
        )
        here = jnp.logical_and(c == lo, c == core)
        gives.append((here, away, pltpu.make_async_copy(src, own, in_sem)))

    pl.semaphore_wait(barrier, len(peers))

    @pl.when(holder)
    def _():
        for here, away, local in gives:
            pl.when(here)(local.start)
            pl.when(jnp.logical_not(here))(away.start)

    gives[0][2].wait()

    def copies(slot):
        mine = xe.at[slot, :, pl.ds(4, 4)]
        ends = (
            (mine, xe.at[slot, :, pl.ds(0, 4)], up_x),
            (mine, xe.at[slot, :, pl.ds(8, 4)], down_x),
            (sy.at[slot, 1], ry.at[slot, 1], up_y),
            (sy.at[slot, 0], ry.at[slot, 0], down_y),
        )
        return [
            pltpu.make_async_remote_copy(
                src_ref=src,
                dst_ref=dst,
                send_sem=send_sem.at[slot, i],
                recv_sem=recv_sem.at[slot, i],
                device_id=device,
                device_id_type=pl.DeviceIdType.MESH,
            )
            for i, (src, dst, device) in enumerate(ends)
        ]

    def send(slot, value=None):
        along = copies(slot)
        if value is None:
            value = [xe[slot, i, 4:8] for i in range(5)]
        else:
            for i in range(5):
                xe[slot, i, 4:8] = value[i]
        for copy in along[:2]:
            copy.start()
        for i in range(5):
            sy[slot, 0, i] = value[i][:, 0:4]
            sy[slot, 1, i] = value[i][:, 4:8]
        for copy in along[2:]:
            copy.start()

    def receive(slot):
        for copy in copies(slot):
            copy.wait_recv()
        for i in range(5):
            yh[slot, i] = jnp.concatenate([ry[slot, 0, i], ry[slot, 1, i]], axis=1)

    def begin(slot):
        return inner([xe[slot, i, 4:8] for i in range(5)])

    def evaluate(slot, into, begun):
        result = outer(begun, *([ref[slot, i, part] for i in range(5)] for ref, part in ((xe, slice(0, 4)), (xe, slice(8, 12)), (yh, slice(0, 4)))))
        for i in range(5):
            g[into, i] = result[i]

    def mix(*terms, base=None):
        parts = []
        for i in range(5):
            total = None if base is None else base[i]
            for kind, slot, factor in terms:
                a = xe[slot, i, 4:8] if kind == "u" else g[slot, i]
                a = a if factor == 1.0 else factor * a
                total = a if total is None else total + a
            parts.append(total)
        return parts

    inside = ((xe, slice(4, 8)),)
    around = ((xe, slice(0, 4)), (xe, slice(8, 12)), (yh, slice(0, 4)))

    def combine(slot, terms, where):
        for ref, part in where:
            for i in range(5):
                total = None
                for source, factor in terms:
                    a = ref[source, i, part]
                    a = a if factor == 1.0 else factor * a
                    total = a if total is None else total + a
                ref[slot, i, part] = total

    def place(level):
        return out.at[0, :, pl.ds(4 * c, 4), pl.ds(rows, 8), :]

    def final(level, src):
        piece_sem = orecv_sem.at[(pos % 2) * 2 + c]
        here = jnp.logical_and(jnp.logical_and(y == level, c == lo), lo == back)
        away = pltpu.make_async_remote_copy(
            src_ref=src,
            dst_ref=place(level),
            send_sem=osend_sem.at[level],
            recv_sem=piece_sem,
            device_id=(level, mine_x, h * 2 + lo),
            device_id_type=pl.DeviceIdType.MESH,
        )
        local = pltpu.make_async_copy(src, place(level), piece_sem)

        @pl.when(here)
        def _():
            local.start()

        @pl.when(jnp.logical_not(here))
        def _():
            away.start()

        return here, away

    send(S)
    begun = begin(S)
    receive(S)
    evaluate(S, F0, begun)
    send(U01, mix(("u", S, 1.0), ("g", F0, DT)))
    begun = begin(U01)
    receive(U01)
    evaluate(U01, TA1, begun)
    send(U02, mix(("u", U01, 1.0), ("g", TA1, DT)))
    halves = ((S, 0.5), (U02, 0.5))
    combine(U11, halves, inside)
    begun = begin(U02), begin(U11)
    half_way = mix(("u", S, 1.0), ("g", F0, 0.5 * DT))
    receive(U02)
    evaluate(U02, TA2, begun[0])
    send(U03, mix(("u", U02, 1.0), ("g", TA2, DT)))
    combine(U11, halves, around)
    evaluate(U11, TB1, begun[1])
    send(U21, mix(("g", TB1, 0.5 * DT), base=half_way))
    finals = [final(0, xe.at[U03, :, pl.ds(4, 4)])]
    old = ((S, -5 / 12), (U01, -9 / 12), (U02, -3 / 12))
    new = ((U12, 1.0), (U03, 5 / 12), (U21, 2.0))
    combine(U12, old, inside + around)
    combine(U12, new, inside)
    begun = begin(U03), begin(U21), begin(U12)
    half_way = mix(("u", S, 1.0), ("g", F0, 0.5 * DT))
    base22 = mix(("u", U21, 1.0), ("g", TB1, -4 / 12 * DT), ("g", F0, -1 / 12 * DT))
    base13 = mix(("u", U12, 1.0), ("g", TA2, -4 / 12 * DT), ("g", TA1, -1 / 12 * DT))
    receive(U03)
    evaluate(U03, TA3, begun[0])
    base13 = mix(("g", TA3, 5 / 12 * DT), base=base13)
    receive(U21)
    evaluate(U21, TC1, begun[1])
    send(U31, mix(("g", TC1, 0.5 * DT), base=half_way))
    combine(U12, new, around)
    base22 = mix(("g", TC1, DT), base=base22)
    evaluate(U12, TB2, begun[2])
    send(U22, mix(("g", TB2, 5 / 12 * DT), base=base22))
    send(U13, mix(("g", TB2, DT), base=base13))
    finals.append(final(1, xe.at[U13, :, pl.ds(4, 4)]))
    begun = begin(U31), begin(U22), begin(U13)
    base32 = mix(("u", U31, 1.0), ("g", TC1, -4 / 12 * DT), ("g", F0, -1 / 12 * DT))
    base23 = mix(("u", U22, 1.0), ("g", TB2, -4 / 12 * DT), ("g", TB1, -1 / 12 * DT))
    receive(U31)
    evaluate(U31, TD1, begun[0])
    base32 = mix(("g", TD1, DT), base=base32)
    receive(U22)
    evaluate(U22, TC2, begun[1])
    send(U32, mix(("g", TC2, 5 / 12 * DT), base=base32))
    base23 = mix(("g", TC2, DT), base=base23)
    receive(U13)
    evaluate(U13, TB3, begun[2])
    send(U23, mix(("g", TB3, 5 / 12 * DT), base=base23))
    finals.append(final(2, xe.at[U23, :, pl.ds(4, 4)]))
    begun = begin(U32), begin(U23)
    base33 = mix(("u", U32, 1.0), ("g", TC2, -4 / 12 * DT), ("g", TC1, -1 / 12 * DT))
    receive(U32)
    evaluate(U32, TD2, begun[0])
    base33 = mix(("g", TD2, DT), base=base33)
    receive(U23)
    evaluate(U23, TC3, begun[1])
    last = mix(("g", TC3, 5 / 12 * DT), base=base33)
    for i in range(5):
        fin[i] = last[i]
    finals.append(final(3, fin))

    for slot in range(SENT):
        for copy in copies(slot):
            copy.wait_send()
    for here, away in finals:

        @pl.when(jnp.logical_not(here))
        def _(away=away):
            away.wait_send()

    @pl.when(holder)
    def _():
        for here, away, _ in gives:
            pl.when(jnp.logical_not(here))(away.wait_send)

    for i in range(4):
        pltpu.make_async_copy(fin, place(3), orecv_sem.at[i]).wait()


def solution(mesh):
    nxp, nzh = mesh.shape["gx"] // 2, mesh.shape["gy"] // 2

    def body(state):
        f32 = jnp.float32
        return pl.pallas_call(
            lambda *refs: kernel(nxp, nzh, *refs),
            out_shape=jax.ShapeDtypeStruct((1,) + state.shape, f32),
            in_specs=[pl.BlockSpec(memory_space=pltpu.HBM)],
            out_specs=pl.BlockSpec(memory_space=OUT_SPACE),
            scratch_shapes=[
                pltpu.VMEM((12, 5, 12, 8, 128), f32),
                pltpu.VMEM((SENT, 2, 5, 4, 4, 128), f32),
                pltpu.VMEM((SENT, 2, 5, 4, 4, 128), f32),
                pltpu.VMEM((12, 5, 4, 8, 128), f32),
                pltpu.VMEM((12, 5, 4, 8, 128), f32),
                pltpu.VMEM((5, 4, 8, 128), f32),
                pltpu.SemaphoreType.DMA,
                pltpu.SemaphoreType.DMA((SENT, 4)),
                pltpu.SemaphoreType.DMA((SENT, 4)),
                pltpu.SemaphoreType.DMA((6,)),
                pltpu.SemaphoreType.DMA((4,)),
            ],
            compiler_params=pltpu.CompilerParams(collective_id=0, vmem_limit_bytes=24 * 2**20, has_side_effects=True),
            name="window",
        )(pltpu.with_memory_space_constraint(state, pltpu.HBM))

    return jax.shard_map(
        body,
        mesh=mesh,
        in_specs=(P(None, "gx", "gy", None),),
        out_specs=P("level", None, "gx", "gy", None),
        check_vma=False,
    )


OUT_SPACE = pl.ANY
```

```python
import jax
import jax.numpy as jnp
from jax import lax
from jax.experimental import pallas as pl
from jax.experimental.pallas import tpu as pltpu
from jax.sharding import PartitionSpec as P

DT = 0.1
A1 = (4.0 / 5.0, -1.0 / 5.0, 4.0 / 105.0, -1.0 / 280.0)
B0 = -205.0 / 72.0
B1 = (8.0 / 5.0, -1.0 / 5.0, 8.0 / 315.0, -1.0 / 560.0)
MU = 0.1

S, U01, U02, U03, U21, U31, U22, U13, U32, U23, U11, U12 = range(12)
SENT = 10
F0, TA1, TA2, TA3, TB1, TB2, TB3, TC1, TC2, TC3, TD1, TD2 = range(12)


def primitives(u):
    rho, m, e = u[0], u[1:4], u[4]
    inv = 1.0 / rho
    v = [mi * inv for mi in m]
    k = 0.5 * (v[0] * v[0] + v[1] * v[1] + v[2] * v[2])
    p = 0.4 * (e - rho * k)
    return m, v, p, e + p, k + p * inv


def flux(parts, d):
    m, v, p, h, _ = parts
    return [m[d]] + [m[i] * v[d] + p if i == d else m[i] * v[d] for i in range(3)] + [h * v[d]]


def diffused(parts):
    return [None, *parts[1], parts[4]]


def along(total, f, w, shifts):
    for n in (1, 2, 3, 4):
        up, down = shifts(f, n)
        term = (-A1[n - 1]) * (up - down)
        total = term if total is None else total + term
        if w is not None:
            up, down = shifts(w, n)
            total = total + (MU * B1[n - 1]) * (up + down)
    return total


def inner(u):
    parts = primitives(u)
    out = []
    for f, w in zip(flux(parts, 2), diffused(parts)):
        total = None if w is None else (3.0 * MU * B0) * w
        out.append(along(total, f, w, lambda a, n: (pltpu.roll(a, 128 - n, 2), pltpu.roll(a, n, 2))))
    return parts, out


def outer(state, low, high, ends):
    parts, out = state
    row = lax.broadcasted_iota(jnp.int32, (4, 8, 128), 1)
    before, after, edge = primitives(low), primitives(high), primitives(ends)

    def join(a, b, c):
        return None if b is None else jnp.concatenate([a, b, c], axis=0)

    fx = [join(*t) for t in zip(flux(before, 0), flux(parts, 0), flux(after, 0))]
    wx = [join(*t) for t in zip(diffused(before), diffused(parts), diffused(after))]
    out = [along(t, f, w, lambda a, n: (a[4 + n : 8 + n], a[4 - n : 8 - n])) for t, f, w in zip(out, fx, wx)]

    def y_shifts(a, n):
        mine, other = a
        up = pltpu.roll(jnp.where(row < n, other, mine), 8 - n, 1)
        down = pltpu.roll(jnp.where(row >= 8 - n, other, mine), n, 1)
        return up, down

    fy = zip(flux(parts, 1), flux(edge, 1))
    wy = [None if a is None else (a, b) for a, b in zip(diffused(parts), diffused(edge))]
    return [along(t, f, w, y_shifts) for t, f, w in zip(out, fy, wy)]


def kernel(nxp, nzh, state, out, xe, ry, sy, yh, g, fin, in_sem, send_sem, recv_sem, osend_sem, orecv_sem):
    y = lax.axis_index("level")
    gx = lax.axis_index("gx")
    gy = lax.axis_index("gy")
    h, c = gy // 2, gy % 2
    x, lo = gx % nxp, gx // nxp
    q = 1 - y // 2
    back = ((y + 1) // 2 + 1) % 2
    mine_x = back * nxp + x
    pos = q + lo * (3 - 2 * q)
    rows = pl.multiple_of((pos % 2) * 8, 8)
    nyi = 4 * nzh

    def owner(column, index, core):
        h2, pos2 = index // 4, index % 4
        lo2 = pos2 // 2
        q2 = pos2 + lo2 * (3 - 2 * pos2)
        return (2 - q2 + (column // nxp) * (1 - 2 * q2), lo2 * nxp + column % nxp, h2 * 2 + core)

    yi = h * 4 + pos
    nx = 2 * nxp
    up_x = owner((mine_x + c) % nx, yi, 1 - c)
    down_x = owner((mine_x + nx - 1 + c) % nx, yi, 1 - c)
    up_y = owner(mine_x, (yi + 1) % nyi, c)
    down_y = owner(mine_x, (yi + nyi - 1) % nyi, c)
    outer_x = owner((mine_x + nx + 2 * c - 1) % nx, yi, 1 - c)

    barrier = pltpu.get_barrier_semaphore()
    peers = [outer_x, up_y, down_y]
    for d in range(16):
        if d:
            peers.append(((y + d // 4) % 4, ((lo + d // 2 % 2) % 2) * nxp + x, h * 2 + (c + d) % 2))
    for peer in peers:
        pl.semaphore_signal(barrier, inc=1, device_id=peer, device_id_type=pl.DeviceIdType.MESH)

    own = xe.at[S, :, pl.ds(4, 4)]
    give_pos = q + c * (3 - 2 * q)
    holder = lo == back
    gives = []
    for core in (0, 1):
        src = state.at[:, pl.ds(4 * core, 4), pl.ds(pl.multiple_of((give_pos % 2) * 8, 8), 8), :]
        away = pltpu.make_async_remote_copy(
            src_ref=src,
            dst_ref=own,
            send_sem=osend_sem.at[4 + core],
            recv_sem=in_sem,
            device_id=(y, c * nxp + x, h * 2 + core),
            device_id_type=pl.DeviceIdType.MESH,
        )
        here = jnp.logical_and(c == lo, c == core)
        gives.append((here, away, pltpu.make_async_copy(src, own, in_sem)))

    pl.semaphore_wait(barrier, len(peers))

    @pl.when(holder)
    def _():
        for here, away, local in gives:
            pl.when(here)(local.start)
            pl.when(jnp.logical_not(here))(away.start)

    gives[0][2].wait()

    def copies(slot):
        mine = xe.at[slot, :, pl.ds(4, 4)]
        ends = (
            (mine, xe.at[slot, :, pl.ds(0, 4)], up_x),
            (mine, xe.at[slot, :, pl.ds(8, 4)], down_x),
            (sy.at[slot, 1], ry.at[slot, 1], up_y),
            (sy.at[slot, 0], ry.at[slot, 0], down_y),
        )
        return [
            pltpu.make_async_remote_copy(
                src_ref=src,
                dst_ref=dst,
                send_sem=send_sem.at[slot, i],
                recv_sem=recv_sem.at[slot, i],
                device_id=device,
                device_id_type=pl.DeviceIdType.MESH,
            )
            for i, (src, dst, device) in enumerate(ends)
        ]

    def send(slot, value=None):
        along = copies(slot)
        if value is None:
            value = [xe[slot, i, 4:8] for i in range(5)]
        else:
            for i in range(5):
                xe[slot, i, 4:8] = value[i]
        for copy in along[:2]:
            copy.start()
        for i in range(5):
            sy[slot, 0, i] = value[i][:, 0:4]
            sy[slot, 1, i] = value[i][:, 4:8]
        for copy in along[2:]:
            copy.start()

    def receive(slot):
        for copy in copies(slot):
            copy.wait_recv()
        for i in range(5):
            yh[slot, i] = jnp.concatenate([ry[slot, 0, i], ry[slot, 1, i]], axis=1)

    def begin(slot):
        return inner([xe[slot, i, 4:8] for i in range(5)])

    def evaluate(slot, into, begun):
        result = outer(begun, *([ref[slot, i, part] for i in range(5)] for ref, part in ((xe, slice(0, 4)), (xe, slice(8, 12)), (yh, slice(0, 4)))))
        for i in range(5):
            g[into, i] = result[i]

    def mix(*terms, base=None):
        parts = []
        for i in range(5):
            total = None if base is None else base[i]
            for kind, slot, factor in terms:
                a = xe[slot, i, 4:8] if kind == "u" else g[slot, i]
                a = a if factor == 1.0 else factor * a
                total = a if total is None else total + a
            parts.append(total)
        return parts

    inside = ((xe, slice(4, 8)),)
    around = ((xe, slice(0, 4)), (xe, slice(8, 12)), (yh, slice(0, 4)))

    def combine(slot, terms, where):
        for ref, part in where:
            for i in range(5):
                total = None
                for source, factor in terms:
                    a = ref[source, i, part]
                    a = a if factor == 1.0 else factor * a
                    total = a if total is None else total + a
                ref[slot, i, part] = total

    def place(level):
        return out.at[0, :, pl.ds(4 * c, 4), pl.ds(rows, 8), :]

    def final(level, src):
        piece_sem = orecv_sem.at[(pos % 2) * 2 + c]
        here = jnp.logical_and(jnp.logical_and(y == level, c == lo), lo == back)
        away = pltpu.make_async_remote_copy(
            src_ref=src,
            dst_ref=place(level),
            send_sem=osend_sem.at[level],
            recv_sem=piece_sem,
            device_id=(level, mine_x, h * 2 + lo),
            device_id_type=pl.DeviceIdType.MESH,
        )
        local = pltpu.make_async_copy(src, place(level), piece_sem)

        @pl.when(here)
        def _():
            local.start()

        @pl.when(jnp.logical_not(here))
        def _():
            away.start()

        return here, away

    send(S)
    begun = begin(S)
    receive(S)
    evaluate(S, F0, begun)
    send(U01, mix(("u", S, 1.0), ("g", F0, DT)))
    begun = begin(U01)
    receive(U01)
    evaluate(U01, TA1, begun)
    send(U02, mix(("u", U01, 1.0), ("g", TA1, DT)))
    halves = ((S, 0.5), (U02, 0.5))
    combine(U11, halves, inside)
    begun = begin(U02), begin(U11)
    half_way = mix(("u", S, 1.0), ("g", F0, 0.5 * DT))
    receive(U02)
    evaluate(U02, TA2, begun[0])
    send(U03, mix(("u", U02, 1.0), ("g", TA2, DT)))
    combine(U11, halves, around)
    evaluate(U11, TB1, begun[1])
    send(U21, mix(("g", TB1, 0.5 * DT), base=half_way))
    finals = [final(0, xe.at[U03, :, pl.ds(4, 4)])]
    old = ((S, -5 / 12), (U01, -9 / 12), (U02, -3 / 12))
    new = ((U12, 1.0), (U03, 5 / 12), (U21, 2.0))
    combine(U12, old, inside + around)
    combine(U12, new, inside)
    begun = begin(U03), begin(U21), begin(U12)
    half_way = mix(("u", S, 1.0), ("g", F0, 0.5 * DT))
    base22 = mix(("u", U21, 1.0), ("g", TB1, -4 / 12 * DT), ("g", F0, -1 / 12 * DT))
    base13 = mix(("u", U12, 1.0), ("g", TA2, -4 / 12 * DT), ("g", TA1, -1 / 12 * DT))
    receive(U03)
    evaluate(U03, TA3, begun[0])
    base13 = mix(("g", TA3, 5 / 12 * DT), base=base13)
    receive(U21)
    evaluate(U21, TC1, begun[1])
    send(U31, mix(("g", TC1, 0.5 * DT), base=half_way))
    combine(U12, new, around)
    base22 = mix(("g", TC1, DT), base=base22)
    evaluate(U12, TB2, begun[2])
    send(U22, mix(("g", TB2, 5 / 12 * DT), base=base22))
    send(U13, mix(("g", TB2, DT), base=base13))
    finals.append(final(1, xe.at[U13, :, pl.ds(4, 4)]))
    begun = begin(U31), begin(U22), begin(U13)
    base32 = mix(("u", U31, 1.0), ("g", TC1, -4 / 12 * DT), ("g", F0, -1 / 12 * DT))
    base23 = mix(("u", U22, 1.0), ("g", TB2, -4 / 12 * DT), ("g", TB1, -1 / 12 * DT))
    receive(U31)
    evaluate(U31, TD1, begun[0])
    base32 = mix(("g", TD1, DT), base=base32)
    receive(U22)
    evaluate(U22, TC2, begun[1])
    send(U32, mix(("g", TC2, 5 / 12 * DT), base=base32))
    base23 = mix(("g", TC2, DT), base=base23)
    receive(U13)
    evaluate(U13, TB3, begun[2])
    send(U23, mix(("g", TB3, 5 / 12 * DT), base=base23))
    finals.append(final(2, xe.at[U23, :, pl.ds(4, 4)]))
    begun = begin(U32), begin(U23)
    base33 = mix(("u", U32, 1.0), ("g", TC2, -4 / 12 * DT), ("g", TC1, -1 / 12 * DT))
    receive(U32)
    evaluate(U32, TD2, begun[0])
    base33 = mix(("g", TD2, DT), base=base33)
    receive(U23)
    evaluate(U23, TC3, begun[1])
    last = mix(("g", TC3, 5 / 12 * DT), base=base33)
    for i in range(5):
        fin[i] = last[i]
    finals.append(final(3, fin))

    for slot in range(SENT):
        for copy in copies(slot):
            copy.wait_send()
    for here, away in finals:

        @pl.when(jnp.logical_not(here))
        def _(away=away):
            away.wait_send()

    @pl.when(holder)
    def _():
        for here, away, _ in gives:
            pl.when(jnp.logical_not(here))(away.wait_send)

    for i in range(4):
        pltpu.make_async_copy(fin, place(3), orecv_sem.at[i]).wait()


def solution(mesh):
    nxp, nzh = mesh.shape["gx"] // 2, mesh.shape["gy"] // 2

    def body(state):
        f32 = jnp.float32
        return pl.pallas_call(
            lambda *refs: kernel(nxp, nzh, *refs),
            out_shape=jax.ShapeDtypeStruct((1,) + state.shape, f32),
            in_specs=[pl.BlockSpec(memory_space=pltpu.HBM)],
            out_specs=pl.BlockSpec(memory_space=OUT_SPACE),
            scratch_shapes=[
                pltpu.VMEM((12, 5, 12, 8, 128), f32),
                pltpu.VMEM((SENT, 2, 5, 4, 4, 128), f32),
                pltpu.VMEM((SENT, 2, 5, 4, 4, 128), f32),
                pltpu.VMEM((12, 5, 4, 8, 128), f32),
                pltpu.VMEM((12, 5, 4, 8, 128), f32),
                pltpu.VMEM((5, 4, 8, 128), f32),
                pltpu.SemaphoreType.DMA,
                pltpu.SemaphoreType.DMA((SENT, 4)),
                pltpu.SemaphoreType.DMA((SENT, 4)),
                pltpu.SemaphoreType.DMA((6,)),
                pltpu.SemaphoreType.DMA((4,)),
            ],
            compiler_params=pltpu.CompilerParams(collective_id=0, vmem_limit_bytes=24 * 2**20, has_side_effects=True),
            name="window",
        )(pltpu.with_memory_space_constraint(state, pltpu.HBM))

    return jax.shard_map(
        body,
        mesh=mesh,
        in_specs=(P(None, "gx", "gy", None),),
        out_specs=P("level", None, "gx", "gy", None),
        check_vma=False,
    )


OUT_SPACE = pl.ANY
```

```python
import jax
import jax.numpy as jnp
from jax import lax
from jax.experimental import pallas as pl
from jax.experimental.pallas import tpu as pltpu
from jax.sharding import PartitionSpec as P

DT = 0.1
A1 = (4.0 / 5.0, -1.0 / 5.0, 4.0 / 105.0, -1.0 / 280.0)
B0 = -205.0 / 72.0
B1 = (8.0 / 5.0, -1.0 / 5.0, 8.0 / 315.0, -1.0 / 560.0)
MU = 0.1

S, U01, U02, U03, U21, U31, U22, U13, U32, U23, U11, U12 = range(12)
SENT = 10
F0, TA1, TA2, TA3, TB1, TB2, TB3, TC1, TC2, TC3, TD1, TD2 = range(12)


def primitives(u):
    rho, m, e = u[0], u[1:4], u[4]
    inv = 1.0 / rho
    v = [mi * inv for mi in m]
    k = 0.5 * (v[0] * v[0] + v[1] * v[1] + v[2] * v[2])
    p = 0.4 * (e - rho * k)
    return m, v, p, e + p, k + p * inv


def flux(parts, d):
    m, v, p, h, _ = parts
    return [m[d]] + [m[i] * v[d] + p if i == d else m[i] * v[d] for i in range(3)] + [h * v[d]]


def diffused(parts):
    return [None, *parts[1], parts[4]]


def along(total, f, w, shifts):
    for n in (1, 2, 3, 4):
        up, down = shifts(f, n)
        term = (-A1[n - 1]) * (up - down)
        total = term if total is None else total + term
        if w is not None:
            up, down = shifts(w, n)
            total = total + (MU * B1[n - 1]) * (up + down)
    return total


def inner(u):
    parts = primitives(u)
    out = []
    for f, w in zip(flux(parts, 2), diffused(parts)):
        total = None if w is None else (3.0 * MU * B0) * w
        out.append(along(total, f, w, lambda a, n: (pltpu.roll(a, 128 - n, 2), pltpu.roll(a, n, 2))))
    return parts, out


def outer(state, low, high, ends):
    parts, out = state
    row = lax.broadcasted_iota(jnp.int32, (4, 8, 128), 1)
    before, after, edge = primitives(low), primitives(high), primitives(ends)

    def join(a, b, c):
        return None if b is None else jnp.concatenate([a, b, c], axis=0)

    fx = [join(*t) for t in zip(flux(before, 0), flux(parts, 0), flux(after, 0))]
    wx = [join(*t) for t in zip(diffused(before), diffused(parts), diffused(after))]
    out = [along(t, f, w, lambda a, n: (a[4 + n : 8 + n], a[4 - n : 8 - n])) for t, f, w in zip(out, fx, wx)]

    def y_shifts(a, n):
        mine, other = a
        up = pltpu.roll(jnp.where(row < n, other, mine), 8 - n, 1)
        down = pltpu.roll(jnp.where(row >= 8 - n, other, mine), n, 1)
        return up, down

    fy = zip(flux(parts, 1), flux(edge, 1))
    wy = [None if a is None else (a, b) for a, b in zip(diffused(parts), diffused(edge))]
    return [along(t, f, w, y_shifts) for t, f, w in zip(out, fy, wy)]


def kernel(nxp, nzh, state, out, xe, ry, sy, yh, g, fin, in_sem, send_sem, recv_sem, osend_sem, orecv_sem):
    y = lax.axis_index("level")
    gx = lax.axis_index("gx")
    gy = lax.axis_index("gy")
    h, c = gy // 2, gy % 2
    x, lo = gx % nxp, gx // nxp
    q = 1 - y // 2
    back = ((y + 1) // 2 + 1) % 2
    mine_x = back * nxp + x
    pos = q + lo * (3 - 2 * q)
    rows = pl.multiple_of((pos % 2) * 8, 8)
    nyi = 4 * nzh

    def owner(column, index, core):
        h2, pos2 = index // 4, index % 4
        lo2 = pos2 // 2
        q2 = pos2 + lo2 * (3 - 2 * pos2)
        return (2 - q2 + (column // nxp) * (1 - 2 * q2), lo2 * nxp + column % nxp, h2 * 2 + core)

    yi = h * 4 + pos
    nx = 2 * nxp
    up_x = owner((mine_x + c) % nx, yi, 1 - c)
    down_x = owner((mine_x + nx - 1 + c) % nx, yi, 1 - c)
    up_y = owner(mine_x, (yi + 1) % nyi, c)
    down_y = owner(mine_x, (yi + nyi - 1) % nyi, c)
    outer_x = owner((mine_x + nx + 2 * c - 1) % nx, yi, 1 - c)

    barrier = pltpu.get_barrier_semaphore()
    peers = [outer_x, up_y, down_y]
    for d in range(16):
        if d:
            peers.append(((y + d // 4) % 4, ((lo + d // 2 % 2) % 2) * nxp + x, h * 2 + (c + d) % 2))
    for peer in peers:
        pl.semaphore_signal(barrier, inc=1, device_id=peer, device_id_type=pl.DeviceIdType.MESH)

    own = xe.at[S, :, pl.ds(4, 4)]
    give_pos = q + c * (3 - 2 * q)
    holder = lo == back
    gives = []
    for core in (0, 1):
        src = state.at[:, pl.ds(4 * core, 4), pl.ds(pl.multiple_of((give_pos % 2) * 8, 8), 8), :]
        away = pltpu.make_async_remote_copy(
            src_ref=src,
            dst_ref=own,
            send_sem=osend_sem.at[4 + core],
            recv_sem=in_sem,
            device_id=(y, c * nxp + x, h * 2 + core),
            device_id_type=pl.DeviceIdType.MESH,
        )
        here = jnp.logical_and(c == lo, c == core)
        gives.append((here, away, pltpu.make_async_copy(src, own, in_sem)))

    pl.semaphore_wait(barrier, len(peers))

    @pl.when(holder)
    def _():
        for here, away, local in gives:
            pl.when(here)(local.start)
            pl.when(jnp.logical_not(here))(away.start)

    gives[0][2].wait()

    def copies(slot):
        mine = xe.at[slot, :, pl.ds(4, 4)]
        ends = (
            (mine, xe.at[slot, :, pl.ds(0, 4)], up_x),
            (mine, xe.at[slot, :, pl.ds(8, 4)], down_x),
            (sy.at[slot, 1], ry.at[slot, 1], up_y),
            (sy.at[slot, 0], ry.at[slot, 0], down_y),
        )
        return [
            pltpu.make_async_remote_copy(
                src_ref=src,
                dst_ref=dst,
                send_sem=send_sem.at[slot, i],
                recv_sem=recv_sem.at[slot, i],
                device_id=device,
                device_id_type=pl.DeviceIdType.MESH,
            )
            for i, (src, dst, device) in enumerate(ends)
        ]

    def send(slot, value=None):
        along = copies(slot)
        if value is None:
            value = [xe[slot, i, 4:8] for i in range(5)]
        else:
            for i in range(5):
                xe[slot, i, 4:8] = value[i]
        for i in range(5):
            sy[slot, 0, i] = value[i][:, 0:4]
            sy[slot, 1, i] = value[i][:, 4:8]
        for copy in along[2:]:
            copy.start()
        for copy in along[:2]:
            copy.start()

    def receive(slot):
        for copy in copies(slot):
            copy.wait_recv()
        for i in range(5):
            yh[slot, i] = jnp.concatenate([ry[slot, 0, i], ry[slot, 1, i]], axis=1)

    def begin(slot):
        return inner([xe[slot, i, 4:8] for i in range(5)])

    def evaluate(slot, into, begun):
        result = outer(begun, *([ref[slot, i, part] for i in range(5)] for ref, part in ((xe, slice(0, 4)), (xe, slice(8, 12)), (yh, slice(0, 4)))))
        for i in range(5):
            g[into, i] = result[i]

    def mix(*terms, base=None):
        parts = []
        for i in range(5):
            total = None if base is None else base[i]
            for kind, slot, factor in terms:
                a = xe[slot, i, 4:8] if kind == "u" else g[slot, i]
                a = a if factor == 1.0 else factor * a
                total = a if total is None else total + a
            parts.append(total)
        return parts

    inside = ((xe, slice(4, 8)),)
    around = ((xe, slice(0, 4)), (xe, slice(8, 12)), (yh, slice(0, 4)))

    def combine(slot, terms, where):
        for ref, part in where:
            for i in range(5):
                total = None
                for source, factor in terms:
                    a = ref[source, i, part]
                    a = a if factor == 1.0 else factor * a
                    total = a if total is None else total + a
                ref[slot, i, part] = total

    def place(level):
        return out.at[0, :, pl.ds(4 * c, 4), pl.ds(rows, 8), :]

    def final(level, src):
        piece_sem = orecv_sem.at[(pos % 2) * 2 + c]
        here = jnp.logical_and(jnp.logical_and(y == level, c == lo), lo == back)
        away = pltpu.make_async_remote_copy(
            src_ref=src,
            dst_ref=place(level),
            send_sem=osend_sem.at[level],
            recv_sem=piece_sem,
            device_id=(level, mine_x, h * 2 + lo),
            device_id_type=pl.DeviceIdType.MESH,
        )
        local = pltpu.make_async_copy(src, place(level), piece_sem)

        @pl.when(here)
        def _():
            local.start()

        @pl.when(jnp.logical_not(here))
        def _():
            away.start()

        return here, away

    send(S)
    begun = begin(S)
    receive(S)
    evaluate(S, F0, begun)
    send(U01, mix(("u", S, 1.0), ("g", F0, DT)))
    begun = begin(U01)
    receive(U01)
    evaluate(U01, TA1, begun)
    send(U02, mix(("u", U01, 1.0), ("g", TA1, DT)))
    halves = ((S, 0.5), (U02, 0.5))
    combine(U11, halves, inside)
    begun = begin(U02), begin(U11)
    half_way = mix(("u", S, 1.0), ("g", F0, 0.5 * DT))
    receive(U02)
    evaluate(U02, TA2, begun[0])
    send(U03, mix(("u", U02, 1.0), ("g", TA2, DT)))
    combine(U11, halves, around)
    evaluate(U11, TB1, begun[1])
    send(U21, mix(("g", TB1, 0.5 * DT), base=half_way))
    finals = [final(0, xe.at[U03, :, pl.ds(4, 4)])]
    old = ((S, -5 / 12), (U01, -9 / 12), (U02, -3 / 12))
    new = ((U12, 1.0), (U03, 5 / 12), (U21, 2.0))
    combine(U12, old, inside + around)
    combine(U12, new, inside)
    begun = begin(U03), begin(U21), begin(U12)
    half_way = mix(("u", S, 1.0), ("g", F0, 0.5 * DT))
    base22 = mix(("u", U21, 1.0), ("g", TB1, -4 / 12 * DT), ("g", F0, -1 / 12 * DT))
    base13 = mix(("u", U12, 1.0), ("g", TA2, -4 / 12 * DT), ("g", TA1, -1 / 12 * DT))
    receive(U03)
    evaluate(U03, TA3, begun[0])
    base13 = mix(("g", TA3, 5 / 12 * DT), base=base13)
    receive(U21)
    evaluate(U21, TC1, begun[1])
    send(U31, mix(("g", TC1, 0.5 * DT), base=half_way))
    combine(U12, new, around)
    base22 = mix(("g", TC1, DT), base=base22)
    evaluate(U12, TB2, begun[2])
    send(U22, mix(("g", TB2, 5 / 12 * DT), base=base22))
    send(U13, mix(("g", TB2, DT), base=base13))
    begun = begin(U31), begin(U22), begin(U13)
    base32 = mix(("u", U31, 1.0), ("g", TC1, -4 / 12 * DT), ("g", F0, -1 / 12 * DT))
    base23 = mix(("u", U22, 1.0), ("g", TB2, -4 / 12 * DT), ("g", TB1, -1 / 12 * DT))
    receive(U31)
    evaluate(U31, TD1, begun[0])
    base32 = mix(("g", TD1, DT), base=base32)
    receive(U22)
    evaluate(U22, TC2, begun[1])
    send(U32, mix(("g", TC2, 5 / 12 * DT), base=base32))
    base23 = mix(("g", TC2, DT), base=base23)
    receive(U13)
    finals.append(final(1, xe.at[U13, :, pl.ds(4, 4)]))
    evaluate(U13, TB3, begun[2])
    send(U23, mix(("g", TB3, 5 / 12 * DT), base=base23))
    finals.append(final(2, xe.at[U23, :, pl.ds(4, 4)]))
    begun = begin(U32), begin(U23)
    base33 = mix(("u", U32, 1.0), ("g", TC2, -4 / 12 * DT), ("g", TC1, -1 / 12 * DT))
    receive(U32)
    evaluate(U32, TD2, begun[0])
    base33 = mix(("g", TD2, DT), base=base33)
    receive(U23)
    evaluate(U23, TC3, begun[1])
    last = mix(("g", TC3, 5 / 12 * DT), base=base33)
    for i in range(5):
        fin[i] = last[i]
    finals.append(final(3, fin))

    for slot in range(SENT):
        for copy in copies(slot):
            copy.wait_send()
    for here, away in finals:

        @pl.when(jnp.logical_not(here))
        def _(away=away):
            away.wait_send()

    @pl.when(holder)
    def _():
        for here, away, _ in gives:
            pl.when(jnp.logical_not(here))(away.wait_send)

    for i in range(4):
        pltpu.make_async_copy(fin, place(3), orecv_sem.at[i]).wait()


def solution(mesh):
    nxp, nzh = mesh.shape["gx"] // 2, mesh.shape["gy"] // 2

    def body(state):
        f32 = jnp.float32
        return pl.pallas_call(
            lambda *refs: kernel(nxp, nzh, *refs),
            out_shape=jax.ShapeDtypeStruct((1,) + state.shape, f32),
            in_specs=[pl.BlockSpec(memory_space=pltpu.HBM)],
            out_specs=pl.BlockSpec(memory_space=OUT_SPACE),
            scratch_shapes=[
                pltpu.VMEM((12, 5, 12, 8, 128), f32),
                pltpu.VMEM((SENT, 2, 5, 4, 4, 128), f32),
                pltpu.VMEM((SENT, 2, 5, 4, 4, 128), f32),
                pltpu.VMEM((12, 5, 4, 8, 128), f32),
                pltpu.VMEM((12, 5, 4, 8, 128), f32),
                pltpu.VMEM((5, 4, 8, 128), f32),
                pltpu.SemaphoreType.DMA,
                pltpu.SemaphoreType.DMA((SENT, 4)),
                pltpu.SemaphoreType.DMA((SENT, 4)),
                pltpu.SemaphoreType.DMA((6,)),
                pltpu.SemaphoreType.DMA((4,)),
            ],
            compiler_params=pltpu.CompilerParams(collective_id=0, vmem_limit_bytes=24 * 2**20, has_side_effects=True),
            name="window",
        )(pltpu.with_memory_space_constraint(state, pltpu.HBM))

    return jax.shard_map(
        body,
        mesh=mesh,
        in_specs=(P(None, "gx", "gy", None),),
        out_specs=P("level", None, "gx", "gy", None),
        check_vma=False,
    )


OUT_SPACE = pl.ANY
```
